32 devices in a mesh: ctx: 16 (over z, y, x), fsdp: 2 (over core).
Axes of the slice: x: 2, y: 2, z: 4, core: 2. Of those that a mesh axis runs over, the one named last changes fastest.
Arguments:
- block_input: float32 [2, 2048, 768], P('fsdp', 'ctx'), may hold values from -6 to 6
- cotangent: float32 [2, 2048, 768], P('fsdp', 'ctx'), may hold values from -6 to 6
- block_doc: int32 [2, 32], P('fsdp'), may hold values from 0 to 3, never falling along the last dimension, each value on 1 to 16 neighbouring positions
- assign: int32 [16, 2], replicated, may hold values from 0 to 31, as said below
- ln_gain: float32 [2, 768], replicated, may hold values from 0.1 to 1.9
- ln_bias: float32 [2, 768], replicated, may hold values from -3 to 3
- w_qkv: bfloat16 [768, 2304], P('fsdp'), may hold values from -2.8867513 to 2.8867513
- qv_bias: float32 [2, 768], replicated, may hold values from -2 to 2
- w_out: bfloat16 [768, 768], P('fsdp'), may hold values from -1.25 to 1.25
- res_bias: float32 [2, 768], replicated, may hold values from -2 to 2
- w_fc: bfloat16 [768, 3072], P(None, 'fsdp'), may hold values from -0.21875 to 0.21875
- fc_bias: float32 [3072], replicated, may hold values from -3 to 3
- w_proj: bfloat16 [3072, 768], P('fsdp'), may hold values from -0.109375 to 0.109375
Outputs:
- block_output: float32 [2, 2048, 768], P('fsdp', 'ctx')
- input_grad: float32 [2, 2048, 768], P('fsdp', 'ctx')
- w_qkv_grad: float32 [768, 2304], P('fsdp', 'ctx')
- w_out_grad: float32 [768, 768], P('fsdp', 'ctx')
- w_fc_grad: float32 [768, 3072], P('ctx', 'fsdp')
- w_proj_grad: float32 [3072, 768], P('fsdp', 'ctx')
- ln_gain_grad: float32 [2, 768], replicated
- ln_bias_grad: float32 [2, 768], replicated
- qv_bias_grad: float32 [2, 768], replicated
- fc_bias_grad: float32 [3072], replicated
- res_bias_grad: float32 [2, 768], replicated
The draws below stay inside these ranges and needn't reach their ends.
Inputs may be any that keep to these rules, and one draw needn't show every extreme that they name: `assign`: row c holds a block p below 16 in column 0 and its mirror 2 * 16 - 1 - p in column 1; every block of 0 to 31 stands in exactly one row. `block_doc`: along each sequence's blocks the document number never falls; each of the 4 documents holds at least one block.
All inputs are finite; a program needn't handle non-finite values.
Results may differ from the reference program's by a relative error of at most 0.015.
Values may be sent and summed in bfloat16 or wider, within the bound.
A program may use at most 192 MiB of HBM per device.

```python
import math
import jax
import jax.numpy as jnp
import numpy as np
from jax import lax

D = 768
H = 12
HD = 64
FF = 3072
BLK = 64
DOCS = 4
TOK_DEV = 128
LEN = 2048
NB = 32
SEQS = 2
N_CTX = 16


def draw_assign(key, part):
    order = jax.random.permutation(key, N_CTX).astype(jnp.int32)
    return jnp.stack([order, 2 * N_CTX - 1 - order], axis=1).astype(jnp.int32)


def draw_w_qkv(key, part):
    normal_part = jax.random.truncated_normal(key, -6.0, 6.0, (D, 3 * D), jnp.float32) * D ** (-0.5)
    return normal_part.astype(jnp.bfloat16)


def levels(key, dims, pieces, low, top_value):
    factor_of = 1.0
    for axis_at, shards_of in pieces:
        draws = jax.random.uniform(jax.random.fold_in(jax.random.fold_in(key, 6), axis_at), (shards_of,), jnp.float32, low / len(pieces), top_value / len(pieces))
        factor_of = factor_of * jnp.repeat(jnp.exp(draws), dims[axis_at] // shards_of).reshape((-1,) + (1,) * (len(dims) - 1 - axis_at))
    return factor_of


def profile(number_of, total, bound, slope):
    loads = [(1 << 20) // math.isqrt(rank ** slope) + 1 for rank in range(2, number_of + 1)]
    spare, counts = total - bound - (number_of - 1), [1] * (number_of - 1)
    while spare > 0:
        free = [i for i in range(number_of - 1) if counts[i] < bound]
        whole, remaining = sum([loads[i] for i in free]), spare
        for i in free:
            more = min(bound - counts[i], max(1, remaining * loads[i] // whole), spare)
            counts[i] = counts[i] + more
            spare = spare - more
    return np.array([bound] + counts)


def ragged(own_key, count, total, most, skew):
    if count == 2:
        one = jax.random.randint(own_key, (), max(1, total - most), min(most, total - 1) + 1)
        return jnp.stack([one, total - one])
    tallies = jnp.asarray(profile(count, total, most, skew), jnp.int32)
    twos = (count - 1) // 2
    source_of, sink = tallies[1:1 + 2 * twos:2], tallies[2:2 + 2 * twos:2]
    margin = jnp.minimum(source_of - 1, most - sink)
    moved = jax.random.randint(jax.random.fold_in(own_key, 1), (twos,), 0, 1 << 20) % (margin + 1)
    tallies = tallies.at[1:1 + 2 * twos:2].set(source_of - moved).at[2:2 + 2 * twos:2].set(sink + moved)
    return tallies[jax.random.permutation(jax.random.fold_in(own_key, 2), count)]


def noise(stream_key, shape, deviation, reach, shards=(), kind=jnp.bfloat16):
    drawn = jax.random.normal(stream_key, shape, jnp.float32) * deviation
    if len(shards) > 0:
        drawn = levels(stream_key, shape, shards, -0.22, 0.18) * drawn
    return jnp.clip(drawn, min=-reach, max=reach).astype(kind)


def setup_inputs(seed: int = 0) -> dict:
    keys = jax.random.split(jax.random.key(seed), 14)
    return {
        "block_input": noise(keys[0], (SEQS, LEN, D), 1.0, 6.0, ((0, 2), (1, 16)), jnp.float32),
        "cotangent": noise(keys[1], (SEQS, LEN, D), 1.0, 6.0, ((0, 2), (1, 16)), jnp.float32),
        "block_doc": jax.vmap(lambda own: jnp.searchsorted(jnp.cumsum(ragged(own, DOCS, NB, NB // 2, 2)), jnp.arange(NB), side="right"))(jax.random.split(keys[2], SEQS)).reshape((SEQS, NB)).astype(jnp.int32),
        "assign": draw_assign(jax.random.fold_in(keys[13], 71), 0),
        "ln_gain": jnp.clip(1.0 + 0.18 * jax.random.normal(keys[4], (2, D), jnp.float32), 0.1, 1.9),
        "ln_bias": noise(keys[5], (2, D), 0.5, 3.0, (), jnp.float32),
        "w_qkv": draw_w_qkv(jax.random.fold_in(keys[13], 71), 0),
        "qv_bias": noise(keys[7], (2, D), 0.3, 2.0, (), jnp.float32),
        "w_out": noise(keys[8], (D, D), (D // 32) ** -0.5, 1.25, ((0, 2),)),
        "res_bias": noise(keys[9], (2, D), 0.3, 2.0, (), jnp.float32),
        "w_fc": noise(keys[10], (D, FF), D ** -0.5, 0.21875, ((1, 2),)),
        "fc_bias": noise(keys[11], (FF,), 0.5, 3.0, (), jnp.float32),
        "w_proj": noise(keys[12], (FF, D), FF ** -0.5, 0.109375, ((0, 2),)),
    }


EPSILON = 1e-05

def layer_norm(values, gain, shift):
    centre = lax.optimization_barrier(jnp.mean(values, axis=-1, keepdims=True))
    centred = values - centre
    spread = lax.optimization_barrier(jnp.mean(centred * centred, axis=-1, keepdims=True))
    return centred * lax.rsqrt(spread + EPSILON) * gain + shift

def gelu_tanh(values):
    return jax.nn.gelu(values, approximate=True)

def matmul(left, right):
    return jnp.dot(left, right, preferred_element_type=jnp.float32)

def rounded(values):
    return lax.optimization_barrier(values.astype(jnp.bfloat16)).astype(jnp.float32)

def reference(block_input, cotangent, block_doc, assign, ln_gain, ln_bias, w_qkv, qv_bias, w_out, res_bias, w_fc, fc_bias, w_proj):
    score_scale = HD ** (-0.5)
    dev_group = math.gcd(4, N_CTX)
    query_rows = dev_group * TOK_DEV
    block_total = LEN // query_rows
    flat_blocks = assign.reshape(-1)
    key_block = jnp.repeat(flat_blocks, BLK)
    positions = key_block * BLK + jnp.arange(LEN, dtype=jnp.int32) % BLK

    def per_sequence(running_total, inputs):
        x_rows, cotangent_rows, doc_ids = inputs
        documents = jnp.repeat(doc_ids[flat_blocks], BLK)
        h_one = layer_norm(x_rows, ln_gain[0], ln_bias[0]).astype(jnp.bfloat16)
        qkv_rows = matmul(h_one, w_qkv)
        queries_f = rounded(qkv_rows[:, :D] + qv_bias[0])
        keys_f = rounded(qkv_rows[:, D:2 * D])
        values_f = rounded(qkv_rows[:, 2 * D:] + qv_bias[1])
        key_heads = keys_f.reshape(LEN, H, HD)
        value_heads = values_f.reshape(LEN, H, HD)

        def scores_of(number):
            row_first = number * query_rows
            query_heads = lax.dynamic_slice_in_dim(queries_f, row_first, query_rows, 0).reshape(query_rows, H, HD)
            query_pos = lax.dynamic_slice_in_dim(positions, row_first, query_rows, 0)
            query_doc = lax.dynamic_slice_in_dim(documents, row_first, query_rows, 0)
            allowed = (positions[None, :] <= query_pos[:, None]) & (documents[None, :] == query_doc[:, None])
            raw_scores = jnp.einsum('qhd,khd->hqk', query_heads, key_heads) * score_scale
            return (query_heads, jnp.where(allowed[None], raw_scores, -jnp.inf))

        def forward_block(number):
            unused, scores = scores_of(number)
            top_score = lax.optimization_barrier(jnp.max(scores, axis=-1, keepdims=True))
            log_total = top_score + jnp.log(lax.optimization_barrier(jnp.sum(jnp.exp(scores - top_score), axis=-1, keepdims=True)))
            prob_b = rounded(jnp.exp(scores - log_total))
            mixed_out = jnp.einsum('hqk,khd->qhd', prob_b, value_heads)
            return (mixed_out.reshape(query_rows, D), log_total[..., 0])
        attn_blocks, lse_blocks = lax.map(forward_block, jnp.arange(block_total, dtype=jnp.int32))
        attn_f = attn_blocks.reshape(LEN, D)
        attn_b = attn_f.astype(jnp.bfloat16)
        mid_rows = x_rows + matmul(attn_b, w_out) + res_bias[0]
        h_two = layer_norm(mid_rows, ln_gain[1], ln_bias[1]).astype(jnp.bfloat16)
        pre_act = matmul(h_two, w_fc) + fc_bias
        hidden = gelu_tanh(pre_act).astype(jnp.bfloat16)
        out_rows = mid_rows + matmul(hidden, w_proj) + res_bias[1]
        grad_out_b = cotangent_rows.astype(jnp.bfloat16)
        projection_gradient = matmul(hidden.T, grad_out_b)
        grad_hidden = matmul(grad_out_b, w_proj.T)
        preactivation_gradient = jax.vjp(gelu_tanh, pre_act)[1](grad_hidden)[0]
        grad_pre_b = preactivation_gradient.astype(jnp.bfloat16)
        expand_gradient = matmul(h_two.T, grad_pre_b)
        grad_normed = matmul(grad_pre_b, w_fc.T)
        mid_from_norm, second_norm_gain, second_norm_bias = jax.vjp(layer_norm, mid_rows, ln_gain[1], ln_bias[1])[1](grad_normed)
        middle_gradient = cotangent_rows + mid_from_norm
        grad_mid_b = middle_gradient.astype(jnp.bfloat16)
        output_gradient = matmul(attn_b.T, grad_mid_b)
        grad_attn_f = rounded(matmul(grad_mid_b, w_out.T))

        def backward_block(sums, number):
            query_heads, scores = scores_of(number)
            row_first = number * query_rows
            prob = jnp.exp(scores - lse_blocks[number][..., None])
            prob_b = rounded(prob)
            grad_heads = lax.dynamic_slice_in_dim(grad_attn_f, row_first, query_rows, 0).reshape(query_rows, H, HD)
            attn_heads = lax.dynamic_slice_in_dim(attn_f, row_first, query_rows, 0).reshape(query_rows, H, HD)
            row_delta = lax.optimization_barrier(jnp.sum(grad_heads * attn_heads, axis=-1)).T
            grad_prob = jnp.einsum('qhd,khd->hqk', grad_heads, value_heads)
            grad_score = rounded(prob * (grad_prob - row_delta[:, :, None]) * score_scale)
            query_gradient_rows = jnp.einsum('hqk,khd->qhd', grad_score, key_heads).reshape(query_rows, D)
            split_score = grad_score.reshape(H, dev_group, TOK_DEV, LEN)
            split_prob = prob_b.reshape(H, dev_group, TOK_DEV, LEN)
            split_query = query_heads.reshape(dev_group, TOK_DEV, H, HD)
            split_grad = grad_heads.reshape(dev_group, TOK_DEV, H, HD)
            key_terms = rounded(jnp.einsum('hgtk,gthd->gkhd', split_score, split_query))
            value_terms = rounded(jnp.einsum('hgtk,gthd->gkhd', split_prob, split_grad))
            key_sum = sums[0] + lax.optimization_barrier(jnp.sum(key_terms, axis=0)).reshape(LEN, D)
            value_sum = sums[1] + lax.optimization_barrier(jnp.sum(value_terms, axis=0)).reshape(LEN, D)
            return ((key_sum, value_sum), query_gradient_rows)
        zeros_pair = (jnp.zeros((LEN, D), jnp.float32), jnp.zeros((LEN, D), jnp.float32))
        (key_grad, value_gradient_rows), query_blocks = lax.scan(backward_block, zeros_pair, jnp.arange(block_total, dtype=jnp.int32))
        query_gradient_rows = query_blocks.reshape(LEN, D)
        grad_qkv_b = jnp.concatenate([query_gradient_rows, key_grad, value_gradient_rows], axis=1).astype(jnp.bfloat16)
        query_key_value_gradient = matmul(h_one.T, grad_qkv_b)
        grad_normed_one = matmul(grad_qkv_b, w_qkv.T)
        in_from_norm, first_norm_gain, first_norm_bias = jax.vjp(layer_norm, x_rows, ln_gain[0], ln_bias[0])[1](grad_normed_one)
        input_rows = middle_gradient + in_from_norm
        summand_terms = (query_key_value_gradient, output_gradient, expand_gradient, projection_gradient, jnp.stack([first_norm_gain, second_norm_gain]), jnp.stack([first_norm_bias, second_norm_bias]), jnp.stack([lax.optimization_barrier(jnp.sum(query_gradient_rows, axis=0)), lax.optimization_barrier(jnp.sum(value_gradient_rows, axis=0))]), lax.optimization_barrier(jnp.sum(preactivation_gradient, axis=0)), jnp.stack([lax.optimization_barrier(jnp.sum(middle_gradient, axis=0)), lax.optimization_barrier(jnp.sum(cotangent_rows, axis=0))]))
        updated_state = tuple((prior_state + summand_term for prior_state, summand_term in zip(running_total, summand_terms)))
        return (updated_state, (out_rows, input_rows))
    start_totals = (jnp.zeros((D, 3 * D), jnp.float32), jnp.zeros((D, D), jnp.float32), jnp.zeros((D, FF), jnp.float32), jnp.zeros((FF, D), jnp.float32), jnp.zeros((2, D), jnp.float32), jnp.zeros((2, D), jnp.float32), jnp.zeros((2, D), jnp.float32), jnp.zeros((FF,), jnp.float32), jnp.zeros((2, D), jnp.float32))
    grand, (outputs, input_grads) = lax.scan(per_sequence, start_totals, (block_input, cotangent, block_doc))
    return (outputs, input_grads, grand[0], grand[1], grand[2], grand[3], grand[4], grand[5], grand[6], grand[7], grand[8])
```

```python
import functools

import jax
import jax.numpy as jnp
from jax import lax
from jax.experimental import pallas as pl
from jax.experimental.pallas import tpu as pltpu
from jax.sharding import PartitionSpec as P

HD = 64
EPSILON = 1e-05
MASKED = -1e30
BF = jnp.bfloat16
F32 = jnp.float32


def layer_norm(values, gain, shift):
    centre = jnp.mean(values, axis=-1, keepdims=True)
    centred = values - centre
    spread = jnp.mean(centred * centred, axis=-1, keepdims=True)
    return centred * lax.rsqrt(spread + EPSILON) * gain + shift


def gelu_tanh(values):
    return jax.nn.gelu(values, approximate=True)


def dot(a, b, ca, cb):
    return lax.dot_general(a, b, (((ca,), (cb,)), ((), ())), preferred_element_type=F32)


def exchange_kernel(n, heads, to_heads, x_ref, o_ref, send_sem, recv_sem, own_sem):
    me = lax.axis_index("ctx")
    barrier = pltpu.get_barrier_semaphore()
    for d in range(1, n):
        pl.semaphore_signal(
            barrier,
            inc=1,
            device_id={"ctx": lax.rem(me + d, n)},
            device_id_type=pl.DeviceIdType.MESH,
        )
    pl.semaphore_wait(barrier, n - 1)

    def copy(d):
        peer = lax.rem(me + d, n)
        return pltpu.make_async_remote_copy(
            src_ref=x_ref.at[peer],
            dst_ref=o_ref.at[me],
            send_sem=send_sem.at[d],
            recv_sem=recv_sem.at[d],
            device_id={"ctx": peer},
            device_id_type=pl.DeviceIdType.MESH,
        )

    def arrival(d):
        source = lax.rem(me + n - d, n)
        return pltpu.make_async_remote_copy(
            src_ref=o_ref.at[source],
            dst_ref=o_ref.at[source],
            send_sem=send_sem.at[d],
            recv_sem=recv_sem.at[d],
            device_id={"ctx": source},
            device_id_type=pl.DeviceIdType.MESH,
        )

    for d in range(1, n):
        sends = lax.rem(me + d, n) < heads if to_heads else me < heads

        @pl.when(sends)
        def _():
            copy(d).start()

    @pl.when(me < heads)
    def _():
        own = pltpu.make_async_copy(x_ref.at[me], o_ref.at[me], own_sem)
        own.start()
        own.wait()

    for d in range(1, n):
        receives = me < heads if to_heads else lax.rem(me + n - d, n) < heads

        @pl.when(receives)
        def _():
            arrival(d).wait_recv()

    for d in range(1, n):
        sends = lax.rem(me + d, n) < heads if to_heads else me < heads

        @pl.when(sends)
        def _():
            copy(d).wait_send()


def exchange(x, n, heads, to_heads, number):
    out = jax.ShapeDtypeStruct((n if to_heads else heads,) + x.shape[1:], x.dtype)
    size = x.size * 2
    return pl.pallas_call(
        functools.partial(exchange_kernel, n, heads, to_heads),
        out_shape=out,
        in_specs=[pl.BlockSpec(memory_space=pltpu.VMEM)],
        out_specs=pl.BlockSpec(memory_space=pltpu.VMEM),
        scratch_shapes=[
            pltpu.SemaphoreType.DMA((n,)),
            pltpu.SemaphoreType.DMA((n,)),
            pltpu.SemaphoreType.DMA,
        ],
        cost_estimate=pl.CostEstimate(flops=0, bytes_accessed=40 * size, transcendentals=0),
        compiler_params=pltpu.CompilerParams(collective_id=number, has_side_effects=True),
    )(x)


def forward_kernel(n, tile, x_ref, kpos_ref, qpos_ref, qlow_ref, o_ref, of_ref, lse_ref, k_s, v_s):
    tok = x_ref.shape[2]
    for c in range(n):
        cols = slice(c * tok, (c + 1) * tok)
        k_s[:, cols] = x_ref[c, HD : 2 * HD, :]
        v_s[:, cols] = x_ref[c, 2 * HD :, :]
    kpos = kpos_ref[...]
    per = tile // tok
    for t in range(n // per):
        cols = slice(t * tile, (t + 1) * tile)
        q = jnp.concatenate([x_ref[t * per + i, :HD, :] for i in range(per)], axis=1)
        q = q * jnp.asarray(HD ** (-0.5), BF)
        s = dot(k_s[...], q, 0, 0)
        ok = (kpos <= qpos_ref[:, cols]) & (kpos >= qlow_ref[:, cols])
        s = jnp.where(ok, s, MASKED)
        top = jnp.max(s, axis=0, keepdims=True)
        p = jnp.exp(s - top)
        total = jnp.sum(p, axis=0, keepdims=True)
        lse_ref[:, cols] = top + jnp.log(total)
        out = dot(v_s[...], p.astype(BF), 1, 0) / total
        of_ref[:, cols] = out
        for i in range(per):
            o_ref[t * per + i] = out[:, i * tok : (i + 1) * tok].astype(BF)


def backward_kernel(
    n, tile, x_ref, g_ref, of_ref, lse_ref, kpos_ref, qpos_ref, qlow_ref, o_ref, k_s, v_s, dk_s, dv_s
):
    tok = x_ref.shape[2]
    scale = HD ** (-0.5)
    for c in range(n):
        cols = slice(c * tok, (c + 1) * tok)
        k_s[:, cols] = x_ref[c, HD : 2 * HD, :]
        v_s[:, cols] = x_ref[c, 2 * HD :, :]
    kpos = kpos_ref[...]
    per = tile // tok
    for t in range(n // per):
        cols = slice(t * tile, (t + 1) * tile)
        q = jnp.concatenate([x_ref[t * per + i, :HD, :] for i in range(per)], axis=1)
        q = q * jnp.asarray(scale, BF)
        g = jnp.concatenate([g_ref[t * per + i] for i in range(per)], axis=1)
        delta = jnp.sum(g.astype(F32) * of_ref[:, cols], axis=0, keepdims=True)
        s = dot(k_s[...], q, 0, 0)
        ok = (kpos <= qpos_ref[:, cols]) & (kpos >= qlow_ref[:, cols])
        p = jnp.exp(jnp.where(ok, s - lse_ref[:, cols], MASKED))
        dp = dot(v_s[...], g, 0, 0)
        ds = (p * (dp - delta)).astype(BF)
        dv = dot(g, p.astype(BF), 1, 1)
        dk = dot(q, ds, 1, 1)
        dq = dot(k_s[...], ds, 1, 0) * scale
        if t == 0:
            dk_s[...] = dk
            dv_s[...] = dv
        else:
            dk_s[...] += dk
            dv_s[...] += dv
        for i in range(per):
            o_ref[t * per + i, :HD, :] = dq[:, i * tok : (i + 1) * tok].astype(BF)
    for c in range(n):
        cols = slice(c * tok, (c + 1) * tok)
        o_ref[c, HD : 2 * HD, :] = dk_s[:, cols].astype(BF)
        o_ref[c, 2 * HD :, :] = dv_s[:, cols].astype(BF)


def whole_specs(count):
    return [pl.BlockSpec(memory_space=pltpu.VMEM)] * count


def attention_forward(x, kpos, qpos, qlow):
    n, _, tok = x.shape
    seq = n * tok
    return pl.pallas_call(
        functools.partial(forward_kernel, n, 2 * tok),
        out_shape=(
            jax.ShapeDtypeStruct((n, HD, tok), BF),
            jax.ShapeDtypeStruct((HD, seq), F32),
            jax.ShapeDtypeStruct((1, seq), F32),
        ),
        in_specs=whole_specs(4),
        out_specs=tuple(whole_specs(3)),
        scratch_shapes=[pltpu.VMEM((HD, seq), BF)] * 2,
        cost_estimate=pl.CostEstimate(
            flops=16 * seq * seq * HD, bytes_accessed=seq * HD * 16, transcendentals=seq * seq
        ),
    )(x, kpos, qpos, qlow)


def attention_backward(x, g, attn_f, lse, kpos, qpos, qlow):
    n, _, tok = x.shape
    seq = n * tok
    return pl.pallas_call(
        functools.partial(backward_kernel, n, 2 * tok),
        out_shape=jax.ShapeDtypeStruct(x.shape, BF),
        in_specs=whole_specs(7),
        out_specs=pl.BlockSpec(memory_space=pltpu.VMEM),
        scratch_shapes=[pltpu.VMEM((HD, seq), BF)] * 2 + [pltpu.VMEM((HD, seq), F32)] * 2,
        cost_estimate=pl.CostEstimate(
            flops=40 * seq * seq * HD, bytes_accessed=seq * HD * 24, transcendentals=seq * seq
        ),
    )(x, g, attn_f, lse, kpos, qpos, qlow)


def shift(x, d):
    n = lax.axis_size("fsdp")
    return lax.ppermute(x, "fsdp", [((i + d) % n, i) for i in range(n)])


def gather_ring(x):
    return [x] + [shift(x, d) for d in range(1, lax.axis_size("fsdp"))]


def return_ring(chunks):
    n = lax.axis_size("fsdp")
    total = chunks[0]
    for d in range(1, n):
        total = total + shift(chunks[d].astype(BF), n - d).astype(F32)
    return total


def full_rows(x):
    n = lax.axis_size("fsdp")
    me = lax.axis_index("fsdp")
    parts = gather_ring(x)
    if n == 2:
        first = me == 0
        return jnp.concatenate(
            [jnp.where(first, parts[0], parts[1]), jnp.where(first, parts[1], parts[0])], axis=0
        )
    full = jnp.zeros((n * x.shape[0],) + x.shape[1:], x.dtype)
    for d in range(n):
        full = lax.dynamic_update_slice_in_dim(full, parts[d], ((me + d) % n) * x.shape[0], 0)
    return full


def bits_of(n):
    return n.bit_length() - 1


def scatter_ctx(x, order):
    n = lax.axis_size("ctx")
    count = bits_of(n)
    me = lax.axis_index("ctx")
    rows = x.shape[1:]
    x = x.reshape((2,) * count + rows)
    for step, bit in enumerate(order):
        axis = count - 1 - bit
        mine = (me >> bit) & 1
        keep = lax.dynamic_index_in_dim(x, mine, axis, keepdims=True)
        give = lax.dynamic_index_in_dim(x, 1 - mine, axis, keepdims=True)
        got = lax.ppermute(give, "ctx", [(i, i ^ (1 << bit)) for i in range(n)])
        x = keep.astype(F32) + got.astype(F32)
        if step < count - 1:
            x = x.astype(BF)
    return x.reshape(rows)


def scatter_fsdp_columns(x):
    n = lax.axis_size("fsdp")
    me = lax.axis_index("fsdp")
    width = x.shape[1] // n
    x = x.astype(BF)
    part = lambda d: lax.dynamic_slice_in_dim(x, ((me + d) % n) * width, width, 1)
    return return_ring([part(0).astype(F32)] + [part(d) for d in range(1, n)])


def sum_everywhere(x):
    for name in ("fsdp", "ctx"):
        n = lax.axis_size(name)
        for bit in range(bits_of(n)):
            x = x + lax.ppermute(x, name, [(i, i ^ (1 << bit)) for i in range(n)])
    return x


def body(
    block_input,
    cotangent,
    block_doc,
    assign,
    ln_gain,
    ln_bias,
    w_qkv,
    qv_bias,
    w_out,
    res_bias,
    w_fc,
    fc_bias,
    w_proj,
):
    tokens = block_input.shape[1]
    width = block_input.shape[2]
    block_len = tokens // 2
    heads = width // HD
    ff_total = fc_bias.shape[0]
    ff_local = w_fc.shape[1]
    n = lax.axis_size("ctx")
    groups = lax.axis_size("fsdp")
    seq_len = n * tokens
    order_a = list(range(bits_of(n)))
    order_b = [1, 0] + order_a[2:]
    x_rows = block_input.reshape(tokens, width)
    cotangent_rows = cotangent.reshape(tokens, width)

    doc_ids = block_doc.reshape(-1)
    flat = assign.reshape(-1)
    low_of = jnp.sum(doc_ids[None, :] < doc_ids[:, None], axis=1).astype(jnp.int32) * block_len
    hit = flat[:, None] == jnp.arange(2 * n, dtype=jnp.int32)[None, :]
    low_rows = jnp.sum(jnp.where(hit, low_of[None, :], 0), axis=1)
    pos = (flat[:, None] * block_len + jnp.arange(block_len, dtype=jnp.int32)[None, :]).reshape(-1)
    qpos = pos.reshape(1, seq_len)
    kpos = pos.reshape(seq_len, 1)
    qlow = jnp.broadcast_to(low_rows[:, None], (2 * n, block_len)).reshape(1, seq_len)

    qkv_full = full_rows(w_qkv)
    out_full = full_rows(w_out)
    grad_out_b = cotangent_rows.astype(BF)
    grad_rows = jnp.concatenate(gather_ring(grad_out_b), axis=0)

    h_one = layer_norm(x_rows, ln_gain[0], ln_bias[0]).astype(BF)
    bias_col = jnp.concatenate([qv_bias[0], jnp.zeros((width,), F32), qv_bias[1]])
    qkv_t = (dot(qkv_full, h_one, 0, 1) + bias_col[:, None]).astype(BF)
    by_head = jnp.transpose(qkv_t.reshape(3, heads, HD, tokens), (1, 0, 2, 3)).reshape(
        heads, 3 * HD, tokens
    )
    head_in = exchange(by_head, n, heads, True, 0)
    attn_out, attn_f, lse = attention_forward(head_in, kpos, qpos, qlow)
    attn_t = exchange(attn_out, n, heads, False, 1).reshape(width, tokens)

    mid_rows = x_rows + dot(attn_t, out_full, 0, 0) + res_bias[0]
    h_two = layer_norm(mid_rows, ln_gain[1], ln_bias[1]).astype(BF)
    shard_start = lax.axis_index("fsdp") * ff_local
    h_rows = jnp.concatenate(gather_ring(h_two), axis=0)
    pre_act = dot(h_rows, w_fc, 1, 0) + lax.dynamic_slice_in_dim(fc_bias, shard_start, ff_local, 0)
    hidden = gelu_tanh(pre_act).astype(BF)
    grad_hidden = dot(grad_rows, w_proj, 1, 1)
    grad_pre = jax.vjp(gelu_tanh, pre_act)[1](grad_hidden)[0]
    grad_pre_b = grad_pre.astype(BF)
    back = dot(grad_pre_b, w_fc, 1, 1)
    grad_normed = return_ring([back[d * tokens : (d + 1) * tokens] for d in range(groups)])
    mlp = dot(hidden, w_proj, 1, 0)
    mlp_out = return_ring([mlp[d * tokens : (d + 1) * tokens] for d in range(groups)])
    block_output = mid_rows + mlp_out + res_bias[1]
    fc_local = jnp.sum(grad_pre, axis=0)
    fc_bias_grad = lax.dynamic_update_slice_in_dim(
        jnp.zeros((ff_total,), F32), fc_local, shard_start, 0
    )

    mid_from_norm, second_gain, second_bias = jax.vjp(layer_norm, mid_rows, ln_gain[1], ln_bias[1])[
        1
    ](grad_normed)
    grad_mid = cotangent_rows + mid_from_norm
    grad_mid_b = grad_mid.astype(BF)
    grad_attn_t = dot(out_full, grad_mid_b, 1, 1).astype(BF).reshape(heads, HD, tokens)
    head_grad = exchange(grad_attn_t, n, heads, True, 2)

    proj_grad = dot(grad_rows, hidden, 0, 0).astype(BF).reshape(n, width // n, ff_local)
    fc_grad = dot(h_rows, grad_pre_b, 0, 0).astype(BF).reshape(n, width // n, ff_local)
    out_grad = scatter_fsdp_columns(dot(grad_mid_b, attn_t, 0, 1)).astype(BF)
    proj_shard = scatter_ctx(proj_grad, order_a).T
    fc_shard = scatter_ctx(fc_grad, order_b)
    out_shard = scatter_ctx(out_grad.reshape(n, width // n, width // groups), order_a).T

    head_back = attention_backward(head_in, head_grad, attn_f, lse, kpos, qpos, qlow)
    grad_by_head = exchange(head_back, n, heads, False, 3)
    grad_qkv_t = jnp.transpose(grad_by_head.reshape(heads, 3, HD, tokens), (1, 0, 2, 3)).reshape(
        3 * width, tokens
    )
    qkv_grad = scatter_fsdp_columns(dot(grad_qkv_t, h_one, 1, 0)).astype(BF)
    rows = 3 * width // n
    qkv_grad = qkv_grad.reshape(n, rows, width // groups)
    cut = rows // 2 // 16 * 16
    qkv_shard = jnp.concatenate(
        [scatter_ctx(qkv_grad[:, :cut], order_a), scatter_ctx(qkv_grad[:, cut:], order_b)], axis=0
    ).T
    grad_normed_one = dot(grad_qkv_t, qkv_full, 0, 1)
    in_from_norm, first_gain, first_bias = jax.vjp(layer_norm, x_rows, ln_gain[0], ln_bias[0])[1](
        grad_normed_one
    )
    input_grad = grad_mid + in_from_norm
    qkv_sums = jnp.sum(grad_qkv_t.astype(F32), axis=1).reshape(3, width)
    small = sum_everywhere(
        jnp.concatenate(
            [
                jnp.stack(
                    [
                        first_gain,
                        second_gain,
                        first_bias,
                        second_bias,
                        qkv_sums[0],
                        qkv_sums[2],
                        jnp.sum(grad_mid, axis=0),
                        jnp.sum(cotangent_rows, axis=0),
                    ]
                ),
                fc_bias_grad.reshape(-1, width),
            ],
            axis=0,
        )
    )
    return (
        block_output.reshape(1, tokens, width),
        input_grad.reshape(1, tokens, width),
        qkv_shard,
        out_shard,
        fc_shard,
        proj_shard,
        small[0:2],
        small[2:4],
        small[4:6],
        small[8:].reshape(ff_total),
        small[6:8],
    )


def solution(mesh):
    in_specs = (
        P("fsdp", "ctx", None),
        P("fsdp", "ctx", None),
        P("fsdp", None),
        P(),
        P(),
        P(),
        P("fsdp", None),
        P(),
        P("fsdp", None),
        P(),
        P(None, "fsdp"),
        P(),
        P("fsdp", None),
    )
    out_specs = (
        P("fsdp", "ctx", None),
        P("fsdp", "ctx", None),
        P("fsdp", "ctx"),
        P("fsdp", "ctx"),
        P("ctx", "fsdp"),
        P("fsdp", "ctx"),
        P(),
        P(),
        P(),
        P(),
        P(),
    )
    return jax.shard_map(body, mesh=mesh, in_specs=in_specs, out_specs=out_specs, check_vma=False)
```
